32 devices in a mesh: groups: 2 (over y), corpus: 4 (over z), dp: 4 (over x, core).
Axes of the slice: x: 2, y: 2, z: 4, core: 2. Of those that a mesh axis runs over, the one named last changes fastest.
Arguments:
- hidden_in: bfloat16 [4096, 4096], P(('groups', 'dp'), 'corpus'), parts along dimension 0, may hold values from -6 to 6
- gate_pre: bfloat16 [4096, 14336], P(('groups', 'dp'), 'corpus'), parts along dimension 0, may hold values from -8 to 8
- up_out: bfloat16 [4096, 14336], P(('groups', 'dp'), 'corpus'), parts along dimension 0, may hold values from -6 to 6
- out_grad: bfloat16 [4096, 4096], P(('groups', 'dp'), 'corpus'), parts along dimension 0, may hold values from -6 to 6
- w_down: bfloat16 [14336, 4096], P('corpus', 'dp'), may hold values from -0.09375 to 0.09375
- proj_in: bfloat16 [4096, 64], P('corpus'), may hold values from -0.09375 to 0.09375
- proj_out: bfloat16 [14336, 64], P('corpus'), may hold values from -0.09375 to 0.09375
- lengths: int32 [16], P(('groups', 'dp')), parts along dimension 0, may hold values from 64 to 256, as said below
- slab: bfloat16 [8192, 4096], P(('groups', 'corpus', 'dp')), parts along dimension 0, may hold values from -6 to 6
Outputs:
- query_grads: float32 [16, 4096], P(('groups', 'dp')), parts along dimension 0
- top_means: float32 [16], P(('groups', 'dp')), parts along dimension 0
The draws below stay inside these ranges and needn't reach their ends.
There are 2 independent parts, one for each index of `groups`. The reference program is written for one: setup_inputs(seed, part) draws one part's arguments, and reference() takes and returns one part's arrays. A program takes and returns all parts, laid end to end along the dimension named above; an argument that names none is the same for every part. Nothing has to cross between parts.
Inputs may be any that keep to these rules, and one draw needn't show every extreme that they name: `lengths`: some prompt of every draw uses all 256 positions and some uses 256 // 4.
All inputs are finite; a program needn't handle non-finite values.
Results may differ from the reference program's by a relative error of at most 0.003.
Values may be sent and summed in bfloat16 or wider, within the bound.
A program may use at most 128 MiB of HBM per device.

```python
import math
import jax
import jax.numpy as jnp
from jax import lax

D = 4096
FF = 14336
RANK = 64
TOPK = 16
LENGTH = 256
GRAD = 4096
QUERIES = 8
TOKENS = 2048
CORPUS_ROWS = 4096


def draw_lengths(key, part):
    base = jax.random.randint(key, (QUERIES,), LENGTH // 4, LENGTH + 1)
    longest = jax.random.randint(jax.random.fold_in(key, 7), (), 0, QUERIES)
    shortest = (longest + 1) % QUERIES
    return base.at[longest].set(LENGTH).at[shortest].set(LENGTH // 4).astype(jnp.int32)


def levels(key, dims, cuts, least, high):
    def one(axis_at, parts):
        heights = jax.random.uniform(jax.random.fold_in(jax.random.fold_in(key, 6), axis_at), (parts,), jnp.float32, least / len(cuts), high / len(cuts))
        return jnp.repeat(jnp.exp(heights), dims[axis_at] // parts).reshape((-1,) + (1,) * (len(dims) - axis_at - 1))

    factor_of = one(*cuts[0])
    for cut in cuts[1:]:
        factor_of = factor_of * one(*cut)
    return factor_of


def gaussian(stream_key, shape, spread, reach, cuts=(), held_as=jnp.bfloat16):
    values = spread * jax.random.normal(stream_key, shape, jnp.float32)
    if cuts:
        values = values * levels(stream_key, shape, cuts, -0.22, 0.18)
    return jnp.clip(values, -reach, reach).astype(held_as)


def setup_inputs(seed: int = 0, part: int = 0) -> dict:
    seeds = jax.random.split(jax.random.key(seed), 10)
    part_splits = jax.random.split(jax.random.fold_in(seeds[9], part), 10)
    hidden_in = gaussian(part_splits[0], (TOKENS, D), 1.0, 6.0, ((0, 4), (1, 4)))
    gate_pre = gaussian(part_splits[1], (TOKENS, FF), 1.5, 8.0, ((0, 4), (1, 4)))
    up_out = gaussian(part_splits[2], (TOKENS, FF), 1.0, 6.0, ((0, 4), (1, 4)))
    out_grad = gaussian(part_splits[3], (TOKENS, D), 1.0, 6.0, ((0, 4), (1, 4)))
    w_down = gaussian(seeds[4], (FF, D), D ** -0.5, 0.09375, ((0, 4), (1, 4)))
    proj_in = gaussian(seeds[5], (D, RANK), D ** -0.5, 0.09375, ((0, 4),))
    proj_out = gaussian(seeds[6], (FF, RANK), (FF // 4) ** -0.5, 0.09375, ((0, 4),))
    lengths = draw_lengths(jax.random.fold_in(jax.random.fold_in(seeds[9], part), 71), part)
    slab = gaussian(part_splits[8], (CORPUS_ROWS, GRAD), 1.0, 6.0, ((0, 16),))
    return dict(hidden_in=hidden_in, gate_pre=gate_pre, up_out=up_out, out_grad=out_grad, w_down=w_down, proj_in=proj_in, proj_out=proj_out, lengths=lengths, slab=slab)


def reference(hidden_in, gate_pre, up_out, out_grad, w_down, proj_in, proj_out, lengths, slab):
    hidden_q = hidden_in.reshape(QUERIES, LENGTH, D)
    gate_q = gate_pre.reshape(QUERIES, LENGTH, FF)
    up_q = up_out.reshape(QUERIES, LENGTH, FF)
    grad_q = out_grad.reshape(QUERIES, LENGTH, D)

    def per_prompt(items):
        hidden_rows, gate_rows, up_rows, grad_rows, length_one = items
        grad_hidden = lax.dot_general(grad_rows, w_down, (((1,), (1,)), ((), ())), preferred_element_type=jnp.float32)
        gate_value = gate_rows.astype(jnp.float32)
        sigmoid_gate = jax.nn.sigmoid(gate_value)
        gate_grad = (grad_hidden * up_rows.astype(jnp.float32) * sigmoid_gate * (1.0 + gate_value * (1.0 - sigmoid_gate))).astype(jnp.bfloat16)
        left = jnp.dot(hidden_rows, proj_in, preferred_element_type=jnp.float32)
        right = jnp.dot(gate_grad, proj_out, preferred_element_type=jnp.float32)
        valid_mask = (jnp.arange(LENGTH, dtype=jnp.int32) < length_one).astype(jnp.float32)
        product = jnp.dot((left * valid_mask[:, None]).T, right, precision=lax.Precision.HIGHEST)
        return product.reshape(GRAD)
    query_grads = lax.map(per_prompt, (hidden_q, gate_q, up_q, grad_q, lengths))
    queries = query_grads.astype(jnp.bfloat16)
    scores = lax.dot_general(queries, slab, (((1,), (1,)), ((), ())), preferred_element_type=jnp.float32)
    scores = scores * (4.0 / math.sqrt(GRAD * LENGTH))
    leaders = lax.top_k(scores, TOPK)[0]
    return (query_grads, lax.optimization_barrier(jnp.mean(leaders, axis=1)))
```

```python
import functools
import math

import jax
import jax.numpy as jnp
from jax import lax
from jax.experimental import pallas as pl
from jax.experimental.pallas import tpu as pltpu
from jax.sharding import PartitionSpec as P

TOPK = 16
LENGTH = 256
GRAD = 4096
PIECE = 256
NT = (((1,), (1,)), ((), ()))


def fused_kernel(
    corpus_count,
    hidden_ref, gate_ref, up_ref, og_ref, w_ref, pin_ref, pout_ref,
    left_ref, right_ref,
    wfull, oall, gate_v, up_v, hid_v,
    local_sem, own_s, own_r, xs, xr, ys, yr, sas, sar, sbs, sbr, os_, or_,
):
    g = lax.axis_index("groups")
    c = lax.axis_index("corpus")
    d = lax.axis_index("dp")
    other_g = 1 - g
    sib = d + 1 - 2 * lax.rem(d, 2)
    across = lax.rem(d + 2, 4)
    diag = lax.rem(sib + 2, 4)
    rows = w_ref.shape[0]
    half = rows // 2
    pieces = half // PIECE
    last = corpus_count - 1

    barrier = pltpu.get_barrier_semaphore()

    def greet(where):
        pl.semaphore_signal(
            barrier, inc=1, device_id=where, device_id_type=pl.DeviceIdType.MESH
        )

    greet({"dp": sib})
    greet({"dp": across})
    greet({"groups": other_g})

    for hop in range(1, corpus_count):
        greet({"corpus": lax.rem(c + hop, corpus_count)})

    loads = [
        pltpu.make_async_copy(w_ref, wfull.at[d], local_sem.at[0]),
        pltpu.make_async_copy(og_ref, oall.at[c], local_sem.at[1]),
        pltpu.make_async_copy(gate_ref, gate_v, local_sem.at[2]),
        pltpu.make_async_copy(up_ref, up_v, local_sem.at[3]),
        pltpu.make_async_copy(hidden_ref, hid_v, local_sem.at[4]),
    ]
    pl.semaphore_wait(barrier, 2 + corpus_count)

    def remote(src, dst, ssem, rsem, where):
        return pltpu.make_async_remote_copy(
            src_ref=src, dst_ref=dst, send_sem=ssem, recv_sem=rsem,
            device_id=where, device_id_type=pl.DeviceIdType.MESH,
        )

    def span(side, j):
        return pl.ds(pl.multiple_of(side * half + j * PIECE, PIECE), PIECE)

    def send_x(j):
        return remote(w_ref.at[span(g, j)], wfull.at[d, span(g, j)], xs.at[j], xr.at[j], {"dp": across})

    def got_x(j):
        here = wfull.at[across, span(g, j)]
        return remote(here, here, xs.at[j], xr.at[j], {"dp": across})

    def send_y(j):
        here = wfull.at[across, span(g, j)]
        return remote(here, here, ys.at[j], yr.at[j], {"groups": other_g})

    def got_y(j):
        here = wfull.at[across, span(other_g, j)]
        return remote(here, here, ys.at[j], yr.at[j], {"groups": other_g})

    def send_a(j):
        here = wfull.at[across, span(g, j)]
        return remote(here, here, sas.at[j], sar.at[j], {"dp": sib})

    def got_a(j):
        here = wfull.at[diag, span(g, j)]
        return remote(here, here, sas.at[j], sar.at[j], {"dp": sib})

    def send_b(j):
        here = wfull.at[across, span(other_g, j)]
        return remote(here, here, sbs.at[j], sbr.at[j], {"dp": sib})

    def got_b(j):
        here = wfull.at[diag, span(other_g, j)]
        return remote(here, here, sbs.at[j], sbr.at[j], {"dp": sib})

    send_own = remote(w_ref, wfull.at[d], own_s, own_r, {"dp": sib})
    got_own = remote(w_ref, wfull.at[sib], own_s, own_r, {"dp": sib})

    def up_copy(i):
        block = c - i
        src = og_ref if i == 0 else oall.at[block]
        return remote(src, oall.at[block], os_.at[0, i], or_.at[0, i], {"corpus": c + 1})

    def up_got(i):
        here = oall.at[c - 1 - i]
        return remote(here, here, os_.at[0, i], or_.at[0, i], {"corpus": c - 1})

    def down_copy(i):
        block = c + i
        src = og_ref if i == 0 else oall.at[block]
        return remote(src, oall.at[block], os_.at[1, i], or_.at[1, i], {"corpus": c - 1})

    def down_got(i):
        here = oall.at[c + 1 + i]
        return remote(here, here, os_.at[1, i], or_.at[1, i], {"corpus": c + 1})

    for j in range(pieces):
        send_x(j).start()

    def line_step(i):
        if i > 0:
            @pl.when(c - i >= 0)
            def _():
                up_got(i - 1).wait_recv()

            @pl.when(c + i <= last)
            def _():
                down_got(i - 1).wait_recv()

        if i < last:
            @pl.when((c - i >= 0) & (c < last))
            def _():
                up_copy(i).start()

            @pl.when((c + i <= last) & (c > 0))
            def _():
                down_copy(i).start()

    line_step(0)
    for load in loads:
        load.start()
    send_own.start()
    loads[4].wait()
    left_ref[...] = jnp.dot(hid_v[...], pin_ref[...], preferred_element_type=jnp.float32)

    step = 1
    for j in range(pieces):
        got_x(j).wait_recv()
        send_y(j).start()
        send_a(j).start()
        if j > 0:
            got_y(j - 1).wait_recv()
            send_b(j - 1).start()
        if j % 2 == 1 and step <= last:
            line_step(step)
            step += 1
    while step <= last:
        line_step(step)
        step += 1
    for load in loads[:4]:
        load.wait()
    got_own.wait_recv()
    for j in range(pieces):
        got_a(j).wait_recv()

    right_ref[...] = jnp.zeros_like(right_ref)

    def compute(side, j):
        here = span(side, j)
        total = lax.dot_general(oall[0], wfull[0, here, :], NT, preferred_element_type=jnp.float32)
        for s in range(1, corpus_count):
            total += lax.dot_general(
                oall[s], wfull[s, here, :], NT, preferred_element_type=jnp.float32
            )
        value = gate_v[:, here].astype(jnp.float32)
        sig = 1.0 / (1.0 + jnp.exp(-value))
        grad = total * up_v[:, here].astype(jnp.float32) * sig * (1.0 + value * (1.0 - sig))
        right_ref[...] += jnp.dot(
            grad.astype(jnp.bfloat16), pout_ref[here, :], preferred_element_type=jnp.float32
        )

    @pl.loop(0, pieces)
    def _(j):
        compute(g, j)

    got_y(pieces - 1).wait_recv()
    send_b(pieces - 1).start()
    for j in range(pieces):
        got_b(j).wait_recv()

    @pl.loop(0, pieces)
    def _(j):
        compute(other_g, j)

    send_own.wait_send()
    for j in range(pieces):
        send_x(j).wait_send()
        send_y(j).wait_send()
        send_a(j).wait_send()
        send_b(j).wait_send()
    for i in range(last):
        @pl.when((c - i >= 0) & (c < last))
        def _():
            up_copy(i).wait_send()

        @pl.when((c + i <= last) & (c > 0))
        def _():
            down_copy(i).wait_send()


def fused_parts(corpus_count, hidden_in, gate_pre, up_out, out_grad, w_down, proj_in, proj_out):
    tokens, depth = out_grad.shape
    rows = w_down.shape[0]
    rank = proj_in.shape[1]
    pieces = rows // 2 // PIECE
    dma = pltpu.SemaphoreType.DMA
    anywhere = pl.BlockSpec(memory_space=pl.ANY)
    inside = pl.BlockSpec(memory_space=pltpu.VMEM)
    part = jax.ShapeDtypeStruct((tokens, rank), jnp.float32)
    return pl.pallas_call(
        functools.partial(fused_kernel, corpus_count),
        out_shape=(part, part),
        in_specs=[anywhere] * 5 + [inside] * 2,
        out_specs=(inside, inside),
        scratch_shapes=[
            pltpu.VMEM((4, rows, depth), jnp.bfloat16),
            pltpu.VMEM((corpus_count, tokens, depth), jnp.bfloat16),
            pltpu.VMEM((tokens, rows), jnp.bfloat16),
            pltpu.VMEM((tokens, rows), jnp.bfloat16),
            pltpu.VMEM(hidden_in.shape, jnp.bfloat16),
            dma((5,)), dma, dma,
        ]
        + [dma((pieces,))] * 8
        + [dma((2, corpus_count)), dma((2, corpus_count))],
        compiler_params=pltpu.CompilerParams(
            collective_id=0, has_side_effects=True, vmem_limit_bytes=56 * 1024 * 1024
        ),
    )(hidden_in, gate_pre, up_out, out_grad, w_down, proj_in, proj_out)


def plain_parts(hidden_in, gate_pre, up_out, out_grad, w_down, proj_in, proj_out):
    full_weight = lax.all_gather(w_down, "dp", axis=1, tiled=True)
    grad_hidden = lax.dot_general(
        lax.all_gather(out_grad, "corpus", axis=1, tiled=True),
        full_weight,
        NT,
        preferred_element_type=jnp.float32,
    )
    gate_value = gate_pre.astype(jnp.float32)
    sigmoid_gate = jax.nn.sigmoid(gate_value)
    gate_grad = (
        grad_hidden
        * up_out.astype(jnp.float32)
        * sigmoid_gate
        * (1.0 + gate_value * (1.0 - sigmoid_gate))
    ).astype(jnp.bfloat16)
    left_part = jnp.dot(hidden_in, proj_in, preferred_element_type=jnp.float32)
    right_part = jnp.dot(gate_grad, proj_out, preferred_element_type=jnp.float32)
    return left_part, right_part


def local(fused, corpus_count, hidden_in, gate_pre, up_out, out_grad, w_down, proj_in, proj_out, lengths, slab):
    tok_rows = hidden_in.shape[0]
    query_count = lengths.shape[0]
    layer = (hidden_in, gate_pre, up_out, out_grad, w_down, proj_in, proj_out)
    if fused:
        left_part, right_part = fused_parts(corpus_count, *layer)
    else:
        left_part, right_part = plain_parts(*layer)
    token_index = jnp.arange(tok_rows, dtype=jnp.int32)
    position = token_index % LENGTH
    prompt_of = token_index // LENGTH
    prompt_ids = jnp.arange(query_count, dtype=jnp.int32)
    mask_table = (
        (prompt_of[:, None] == prompt_ids[None, :]) & (position[:, None] < lengths[None, :])
    ).astype(jnp.float32)
    left_all, right_all = lax.psum((left_part, right_part), "corpus")
    example_grads = jnp.einsum(
        "tq,tr,tc->qrc", mask_table, left_all, right_all, precision=lax.Precision.HIGHEST
    )
    query_grads = example_grads.reshape(query_count, GRAD)
    queries = lax.all_gather(query_grads.astype(jnp.bfloat16), "dp", axis=0, tiled=True)
    scores = lax.dot_general(queries, slab, NT, preferred_element_type=jnp.float32)
    scores = scores * (4.0 / math.sqrt(GRAD * LENGTH))
    leaders = lax.top_k(scores, TOPK)[0]
    gathered = lax.all_gather(leaders, ("corpus", "dp"), axis=1, tiled=True)
    leaders = lax.top_k(gathered, TOPK)[0]
    own_rows = lax.dynamic_slice_in_dim(leaders, lax.axis_index("dp") * query_count, query_count, 0)
    return (query_grads, jnp.mean(own_rows, axis=1))


def solution(mesh):
    sizes = dict(mesh.shape)
    fused = sizes["groups"] == 2 and sizes["dp"] == 4 and sizes["corpus"] == 4
    in_specs = (
        P(("groups", "dp"), "corpus"),
        P(("groups", "dp"), "corpus"),
        P(("groups", "dp"), "corpus"),
        P(("groups", "dp"), "corpus"),
        P("corpus", "dp"),
        P("corpus", None),
        P("corpus", None),
        P(("groups", "dp")),
        P(("groups", "corpus", "dp"), None),
    )
    out_specs = (P(("groups", "dp"), None), P(("groups", "dp")))
    return jax.shard_map(
        functools.partial(local, fused, sizes["corpus"]),
        mesh=mesh, in_specs=in_specs, out_specs=out_specs, check_vma=False,
    )
```

```python
import functools
import math

import jax
import jax.numpy as jnp
from jax import lax
from jax.experimental import pallas as pl
from jax.experimental.pallas import tpu as pltpu
from jax.sharding import PartitionSpec as P

TOPK = 16
LENGTH = 256
GRAD = 4096
PIECE = 256
NT = (((1,), (1,)), ((), ()))


def fused_kernel(
    corpus_count,
    hidden_ref, gate_ref, up_ref, og_ref, w_ref, pin_ref, pout_ref,
    out_ref,
    right_ref, wfull, oall, gate_v, up_v, hid_v,
    local_sem, own_s, own_r, xs, xr, ys, yr, sas, sar, sbs, sbr, os_, or_,
):
    g = lax.axis_index("groups")
    c = lax.axis_index("corpus")
    d = lax.axis_index("dp")
    other_g = 1 - g
    sib = d + 1 - 2 * lax.rem(d, 2)
    across = lax.rem(d + 2, 4)
    diag = lax.rem(sib + 2, 4)
    rows = w_ref.shape[0]
    half = rows // 2
    pieces = half // PIECE
    last = corpus_count - 1

    barrier = pltpu.get_barrier_semaphore()

    def greet(where):
        pl.semaphore_signal(
            barrier, inc=1, device_id=where, device_id_type=pl.DeviceIdType.MESH
        )

    greet({"dp": sib})
    greet({"dp": across})
    greet({"groups": other_g})

    for hop in range(1, corpus_count):
        greet({"corpus": lax.rem(c + hop, corpus_count)})

    loads = [
        pltpu.make_async_copy(w_ref, wfull.at[d], local_sem.at[0]),
        pltpu.make_async_copy(og_ref, oall.at[c], local_sem.at[1]),
        pltpu.make_async_copy(gate_ref, gate_v, local_sem.at[2]),
        pltpu.make_async_copy(up_ref, up_v, local_sem.at[3]),
        pltpu.make_async_copy(hidden_ref, hid_v, local_sem.at[4]),
    ]
    pl.semaphore_wait(barrier, 2 + corpus_count)

    def remote(src, dst, ssem, rsem, where):
        return pltpu.make_async_remote_copy(
            src_ref=src, dst_ref=dst, send_sem=ssem, recv_sem=rsem,
            device_id=where, device_id_type=pl.DeviceIdType.MESH,
        )

    def span(side, j):
        return pl.ds(pl.multiple_of(side * half + j * PIECE, PIECE), PIECE)

    def send_x(j):
        return remote(w_ref.at[span(g, j)], wfull.at[d, span(g, j)], xs.at[j], xr.at[j], {"dp": across})

    def got_x(j):
        here = wfull.at[across, span(g, j)]
        return remote(here, here, xs.at[j], xr.at[j], {"dp": across})

    def send_y(j):
        here = wfull.at[across, span(g, j)]
        return remote(here, here, ys.at[j], yr.at[j], {"groups": other_g})

    def got_y(j):
        here = wfull.at[across, span(other_g, j)]
        return remote(here, here, ys.at[j], yr.at[j], {"groups": other_g})

    def send_a(j):
        here = wfull.at[across, span(g, j)]
        return remote(here, here, sas.at[j], sar.at[j], {"dp": sib})

    def got_a(j):
        here = wfull.at[diag, span(g, j)]
        return remote(here, here, sas.at[j], sar.at[j], {"dp": sib})

    def send_b(j):
        here = wfull.at[across, span(other_g, j)]
        return remote(here, here, sbs.at[j], sbr.at[j], {"dp": sib})

    def got_b(j):
        here = wfull.at[diag, span(other_g, j)]
        return remote(here, here, sbs.at[j], sbr.at[j], {"dp": sib})

    send_own = remote(w_ref, wfull.at[d], own_s, own_r, {"dp": sib})
    got_own = remote(w_ref, wfull.at[sib], own_s, own_r, {"dp": sib})

    def up_copy(i):
        block = c - i
        src = og_ref if i == 0 else oall.at[block]
        return remote(src, oall.at[block], os_.at[0, i], or_.at[0, i], {"corpus": c + 1})

    def up_got(i):
        here = oall.at[c - 1 - i]
        return remote(here, here, os_.at[0, i], or_.at[0, i], {"corpus": c - 1})

    def down_copy(i):
        block = c + i
        src = og_ref if i == 0 else oall.at[block]
        return remote(src, oall.at[block], os_.at[1, i], or_.at[1, i], {"corpus": c - 1})

    def down_got(i):
        here = oall.at[c + 1 + i]
        return remote(here, here, os_.at[1, i], or_.at[1, i], {"corpus": c + 1})

    for j in range(pieces):
        send_x(j).start()

    def line_step(i):
        if i > 0:
            @pl.when(c - i >= 0)
            def _():
                up_got(i - 1).wait_recv()

            @pl.when(c + i <= last)
            def _():
                down_got(i - 1).wait_recv()

        if i < last:
            @pl.when((c - i >= 0) & (c < last))
            def _():
                up_copy(i).start()

            @pl.when((c + i <= last) & (c > 0))
            def _():
                down_copy(i).start()

    line_step(0)
    for load in loads:
        load.start()
    send_own.start()
    loads[4].wait()
    rank = pin_ref.shape[0]
    out_ref[:, :rank] = lax.dot_general(
        hid_v[...], pin_ref[...], NT, preferred_element_type=jnp.float32
    )

    step = 1
    for j in range(pieces):
        got_x(j).wait_recv()
        send_y(j).start()
        send_a(j).start()
        if j > 0:
            got_y(j - 1).wait_recv()
            send_b(j - 1).start()
        if j % 2 == 1 and step <= last:
            line_step(step)
            step += 1
    while step <= last:
        line_step(step)
        step += 1
    for load in loads[:4]:
        load.wait()
    got_own.wait_recv()
    for j in range(pieces):
        got_a(j).wait_recv()

    right_ref[...] = jnp.zeros_like(right_ref)

    def compute(side, j):
        here = span(side, j)
        total = lax.dot_general(oall[0], wfull[0, here, :], NT, preferred_element_type=jnp.float32)
        for s in range(1, corpus_count):
            total += lax.dot_general(
                oall[s], wfull[s, here, :], NT, preferred_element_type=jnp.float32
            )
        value = gate_v[:, here].astype(jnp.float32)
        sig = 1.0 / (1.0 + jnp.exp(-value))
        grad = total * up_v[:, here].astype(jnp.float32) * sig * (1.0 + value * (1.0 - sig))
        right_ref[...] += lax.dot_general(
            grad.astype(jnp.bfloat16), pout_ref[:, here], NT, preferred_element_type=jnp.float32
        )

    @pl.loop(0, pieces)
    def _(j):
        compute(g, j)

    got_y(pieces - 1).wait_recv()
    send_b(pieces - 1).start()
    for j in range(pieces):
        got_b(j).wait_recv()

    @pl.loop(0, pieces)
    def _(j):
        compute(other_g, j)

    out_ref[:, rank:] = right_ref[...]
    send_own.wait_send()
    for j in range(pieces):
        send_x(j).wait_send()
        send_y(j).wait_send()
        send_a(j).wait_send()
        send_b(j).wait_send()
    for i in range(last):
        @pl.when((c - i >= 0) & (c < last))
        def _():
            up_copy(i).wait_send()

        @pl.when((c + i <= last) & (c > 0))
        def _():
            down_copy(i).wait_send()


def fused_parts(corpus_count, hidden_in, gate_pre, up_out, out_grad, w_down, proj_in, proj_out):
    tokens, depth = out_grad.shape
    rows = w_down.shape[0]
    rank = proj_in.shape[1]
    pieces = rows // 2 // PIECE
    dma = pltpu.SemaphoreType.DMA
    anywhere = pl.BlockSpec(memory_space=pl.ANY)
    inside = pl.BlockSpec(memory_space=pltpu.VMEM)
    return pl.pallas_call(
        functools.partial(fused_kernel, corpus_count),
        out_shape=jax.ShapeDtypeStruct((tokens, 2 * rank), jnp.float32),
        in_specs=[anywhere] * 5 + [inside] * 2,
        out_specs=inside,
        scratch_shapes=[
            pltpu.VMEM((tokens, rank), jnp.float32),
            pltpu.VMEM((4, rows, depth), jnp.bfloat16),
            pltpu.VMEM((corpus_count, tokens, depth), jnp.bfloat16),
            pltpu.VMEM((tokens, rows), jnp.bfloat16),
            pltpu.VMEM((tokens, rows), jnp.bfloat16),
            pltpu.VMEM(hidden_in.shape, jnp.bfloat16),
            dma((5,)), dma, dma,
        ]
        + [dma((pieces,))] * 8
        + [dma((2, corpus_count)), dma((2, corpus_count))],
        compiler_params=pltpu.CompilerParams(
            collective_id=0, has_side_effects=True, vmem_limit_bytes=56 * 1024 * 1024
        ),
    )(hidden_in, gate_pre, up_out, out_grad, w_down, proj_in.T, proj_out.T)


def tail_kernel(
    corpus_count, dp_count,
    lr_ref, lengths_ref, slab_ref,
    grads_ref, means_ref,
    box1, box2, box3, box4, rows_out,
    s1, r1, s2, r2, s3, r3, s4, r4,
):
    c = lax.axis_index("corpus")
    d = lax.axis_index("dp")
    tokens = lr_ref.shape[0]
    rank = lr_ref.shape[1] // 2
    share = tokens // corpus_count
    per_prompt = LENGTH // share
    prompts = tokens // LENGTH
    mesh_id = pl.DeviceIdType.MESH
    hops = range(1, corpus_count)
    dp_hops = range(1, dp_count)
    everyone = [(i, j) for i in range(corpus_count) for j in range(dp_count) if (i, j) != (0, 0)]

    def c_of(hop):
        return lax.rem(c + hop, corpus_count)

    def d_of(hop):
        return lax.rem(d + hop, dp_count)

    barrier = pltpu.get_barrier_semaphore()
    for i, j in everyone:
        pl.semaphore_signal(
            barrier, inc=1, device_id={"corpus": c_of(i), "dp": d_of(j)}, device_id_type=mesh_id
        )
    pl.semaphore_wait(barrier, len(everyone))

    def remote(src, dst, ssem, rsem, where):
        return pltpu.make_async_remote_copy(
            src_ref=src, dst_ref=dst, send_sem=ssem, recv_sem=rsem,
            device_id=where, device_id_type=mesh_id,
        )

    def part_of(who):
        return lr_ref.at[pl.ds(pl.multiple_of(who * share, share), share)]

    sent = []

    def send(*args):
        copy = remote(*args)
        copy.start()
        sent.append(copy)

    for hop in hops:
        send(part_of(c_of(hop)), box1.at[c], s1.at[hop], r1.at[c], {"corpus": c_of(hop)})
    total = lr_ref[pl.ds(pl.multiple_of(c * share, share), share), :]
    for hop in hops:
        who = c_of(hop)
        remote(box1.at[who], box1.at[who], s1.at[hop], r1.at[who], {"corpus": who}).wait_recv()
        total += box1[who]

    position = lax.rem(c, per_prompt) * share + lax.broadcasted_iota(jnp.int32, (share, rank), 0)
    used = position < lengths_ref[c // per_prompt]
    left = jnp.where(used, total[:, :rank], 0.0)
    box2[c] = lax.dot_general(
        left, total[:, rank:], (((0,), (0,)), ((), ())),
        precision=lax.Precision.HIGHEST, preferred_element_type=jnp.float32,
    )
    for hop in hops:
        send(box2.at[c], box2.at[c], s2.at[hop], r2.at[c], {"corpus": c_of(hop)})
    for hop in hops:
        who = c_of(hop)
        remote(box2.at[who], box2.at[who], s2.at[hop], r2.at[who], {"corpus": who}).wait_recv()

    for q in range(prompts):
        whole = box2[q * per_prompt]
        for k in range(1, per_prompt):
            whole += box2[q * per_prompt + k]
        for r in range(rank):
            grads_ref[q : q + 1, r * rank : (r + 1) * rank] = whole[r : r + 1, :]

    box3[d] = grads_ref[...]
    for hop in dp_hops:
        send(box3.at[d], box3.at[d], s3.at[hop], r3.at[d], {"dp": d_of(hop)})
    for hop in dp_hops:
        who = d_of(hop)
        remote(box3.at[who], box3.at[who], s3.at[hop], r3.at[who], {"dp": who}).wait_recv()
    queries = jnp.concatenate([box3[k] for k in range(dp_count)], axis=0).astype(jnp.bfloat16)
    scores = lax.dot_general(queries, slab_ref[...], NT, preferred_element_type=jnp.float32)
    scores = scores * (4.0 / math.sqrt(GRAD * LENGTH))
    for k in range(dp_count):
        rows_out[k] = scores[k * prompts : (k + 1) * prompts, :]

    slot = c * dp_count + d
    box4[slot] = rows_out[d]
    for n, (i, j) in enumerate(everyone):
        send(
            rows_out.at[d_of(j)], box4.at[slot], s4.at[n], r4.at[slot],
            {"corpus": c_of(i), "dp": d_of(j)},
        )
    for n, (i, j) in enumerate(everyone):
        other = c_of(i) * dp_count + d_of(j)
        here = box4.at[other]
        remote(here, here, s4.at[n], r4.at[other], {"corpus": c_of(i), "dp": d_of(j)}).wait_recv()

    values = jnp.concatenate([box4[k] for k in range(corpus_count * dp_count)], axis=1)
    top = jnp.max(values, axis=1, keepdims=True)
    taken = jnp.zeros((prompts, 1), jnp.float32)
    total = jnp.zeros((prompts, 1), jnp.float32)
    for n in range(TOPK):
        count = jnp.sum((values == top).astype(jnp.float32), axis=1, keepdims=True)
        use = jnp.minimum(count, TOPK - taken)
        total += use * top
        taken += use
        if n < TOPK - 1:
            top = jnp.max(jnp.where(values < top, values, -3e38), axis=1, keepdims=True)
    means_ref[...] = jnp.broadcast_to(total * (1.0 / TOPK), means_ref.shape)
    for copy in sent:
        copy.wait_send()


def fused_tail(corpus_count, dp_count, left_right, lengths, slab):
    tokens, width = left_right.shape
    rank = width // 2
    prompts = lengths.shape[0]
    examples = slab.shape[0]
    dma = pltpu.SemaphoreType.DMA
    everyone = corpus_count * dp_count
    inside = pl.BlockSpec(memory_space=pltpu.VMEM)
    f32 = jnp.float32
    grads, means = pl.pallas_call(
        functools.partial(tail_kernel, corpus_count, dp_count),
        out_shape=(
            jax.ShapeDtypeStruct((prompts, GRAD), f32),
            jax.ShapeDtypeStruct((prompts, 128), f32),
        ),
        in_specs=[inside, pl.BlockSpec(memory_space=pltpu.SMEM), inside],
        out_specs=(inside, inside),
        scratch_shapes=[
            pltpu.VMEM((corpus_count, tokens // corpus_count, width), f32),
            pltpu.VMEM((corpus_count, rank, rank), f32),
            pltpu.VMEM((dp_count, prompts, GRAD), f32),
            pltpu.VMEM((everyone, prompts, examples), f32),
            pltpu.VMEM((dp_count, prompts, examples), f32),
            dma((corpus_count,)), dma((corpus_count,)),
            dma((corpus_count,)), dma((corpus_count,)),
            dma((dp_count,)), dma((dp_count,)),
            dma((everyone,)), dma((everyone,)),
        ],
        compiler_params=pltpu.CompilerParams(
            collective_id=1, has_side_effects=True, vmem_limit_bytes=16 * 1024 * 1024
        ),
    )(left_right, lengths, slab)
    return grads, means[:, 0]


def plain_parts(hidden_in, gate_pre, up_out, out_grad, w_down, proj_in, proj_out):
    full_weight = lax.all_gather(w_down, "dp", axis=1, tiled=True)
    grad_hidden = lax.dot_general(
        lax.all_gather(out_grad, "corpus", axis=1, tiled=True),
        full_weight,
        NT,
        preferred_element_type=jnp.float32,
    )
    gate_value = gate_pre.astype(jnp.float32)
    sigmoid_gate = jax.nn.sigmoid(gate_value)
    gate_grad = (
        grad_hidden
        * up_out.astype(jnp.float32)
        * sigmoid_gate
        * (1.0 + gate_value * (1.0 - sigmoid_gate))
    ).astype(jnp.bfloat16)
    left_part = jnp.dot(hidden_in, proj_in, preferred_element_type=jnp.float32)
    right_part = jnp.dot(gate_grad, proj_out, preferred_element_type=jnp.float32)
    return left_part, right_part


def local(fused, corpus_count, hidden_in, gate_pre, up_out, out_grad, w_down, proj_in, proj_out, lengths, slab):
    tok_rows = hidden_in.shape[0]
    query_count = lengths.shape[0]
    layer = (hidden_in, gate_pre, up_out, out_grad, w_down, proj_in, proj_out)
    if fused:
        left_right = fused_parts(corpus_count, *layer)
        return fused_tail(corpus_count, 4, left_right, lengths, slab)
    left_part, right_part = plain_parts(*layer)
    token_index = jnp.arange(tok_rows, dtype=jnp.int32)
    position = token_index % LENGTH
    prompt_of = token_index // LENGTH
    prompt_ids = jnp.arange(query_count, dtype=jnp.int32)
    mask_table = (
        (prompt_of[:, None] == prompt_ids[None, :]) & (position[:, None] < lengths[None, :])
    ).astype(jnp.float32)
    left_all, right_all = lax.psum((left_part, right_part), "corpus")
    example_grads = jnp.einsum(
        "tq,tr,tc->qrc", mask_table, left_all, right_all, precision=lax.Precision.HIGHEST
    )
    query_grads = example_grads.reshape(query_count, GRAD)
    queries = lax.all_gather(query_grads.astype(jnp.bfloat16), "dp", axis=0, tiled=True)
    scores = lax.dot_general(queries, slab, NT, preferred_element_type=jnp.float32)
    scores = scores * (4.0 / math.sqrt(GRAD * LENGTH))
    leaders = lax.top_k(scores, TOPK)[0]
    gathered = lax.all_gather(leaders, ("corpus", "dp"), axis=1, tiled=True)
    leaders = lax.top_k(gathered, TOPK)[0]
    own_rows = lax.dynamic_slice_in_dim(leaders, lax.axis_index("dp") * query_count, query_count, 0)
    return (query_grads, jnp.mean(own_rows, axis=1))


def solution(mesh):
    sizes = dict(mesh.shape)
    fused = sizes["groups"] == 2 and sizes["dp"] == 4 and sizes["corpus"] == 4
    in_specs = (
        P(("groups", "dp"), "corpus"),
        P(("groups", "dp"), "corpus"),
        P(("groups", "dp"), "corpus"),
        P(("groups", "dp"), "corpus"),
        P("corpus", "dp"),
        P("corpus", None),
        P("corpus", None),
        P(("groups", "dp")),
        P(("groups", "corpus", "dp"), None),
    )
    out_specs = (P(("groups", "dp"), None), P(("groups", "dp")))
    return jax.shard_map(
        functools.partial(local, fused, sizes["corpus"]),
        mesh=mesh, in_specs=in_specs, out_specs=out_specs, check_vma=False,
    )
```

```python
import functools
import math

import jax
import jax.numpy as jnp
from jax import lax
from jax.experimental import pallas as pl
from jax.experimental.pallas import tpu as pltpu
from jax.sharding import PartitionSpec as P

TOPK = 16
LENGTH = 256
GRAD = 4096
PIECE = 128
UNIT = 256
NT = (((1,), (1,)), ((), ()))


def fused_kernel(
    corpus_count,
    hidden_ref, gate_ref, up_ref, og_ref, w_ref, pin_ref, pout_ref,
    out_ref,
    right_ref, wfull, oall, gate_v, up_v, hid_v,
    local_sem, own_s, own_r, xs, xr, ys, yr, sas, sar, sbs, sbr, os_, or_,
):
    g = lax.axis_index("groups")
    c = lax.axis_index("corpus")
    d = lax.axis_index("dp")
    other_g = 1 - g
    sib = d + 1 - 2 * lax.rem(d, 2)
    across = lax.rem(d + 2, 4)
    diag = lax.rem(sib + 2, 4)
    rows = w_ref.shape[0]
    half = rows // 2
    pieces = half // PIECE
    last = corpus_count - 1

    barrier = pltpu.get_barrier_semaphore()

    def greet(where):
        pl.semaphore_signal(
            barrier, inc=1, device_id=where, device_id_type=pl.DeviceIdType.MESH
        )

    greet({"dp": sib})
    greet({"dp": across})
    greet({"groups": other_g})

    for hop in range(1, corpus_count):
        greet({"corpus": lax.rem(c + hop, corpus_count)})

    loads = [
        pltpu.make_async_copy(w_ref, wfull.at[d], local_sem.at[0]),
        pltpu.make_async_copy(og_ref, oall.at[c], local_sem.at[1]),
        pltpu.make_async_copy(gate_ref, gate_v, local_sem.at[2]),
        pltpu.make_async_copy(up_ref, up_v, local_sem.at[3]),
        pltpu.make_async_copy(hidden_ref, hid_v, local_sem.at[4]),
    ]
    pl.semaphore_wait(barrier, 2 + corpus_count)

    def remote(src, dst, ssem, rsem, where):
        return pltpu.make_async_remote_copy(
            src_ref=src, dst_ref=dst, send_sem=ssem, recv_sem=rsem,
            device_id=where, device_id_type=pl.DeviceIdType.MESH,
        )

    def span(side, j):
        return pl.ds(pl.multiple_of(side * half + j * PIECE, PIECE), PIECE)

    def send_x(j):
        return remote(w_ref.at[span(g, j)], wfull.at[d, span(g, j)], xs.at[j], xr.at[j], {"dp": across})

    def got_x(j):
        here = wfull.at[across, span(g, j)]
        return remote(here, here, xs.at[j], xr.at[j], {"dp": across})

    def send_y(j):
        here = wfull.at[across, span(g, j)]
        return remote(here, here, ys.at[j], yr.at[j], {"groups": other_g})

    def got_y(j):
        here = wfull.at[across, span(other_g, j)]
        return remote(here, here, ys.at[j], yr.at[j], {"groups": other_g})

    def send_a(j):
        here = wfull.at[across, span(g, j)]
        return remote(here, here, sas.at[j], sar.at[j], {"dp": sib})

    def got_a(j):
        here = wfull.at[diag, span(g, j)]
        return remote(here, here, sas.at[j], sar.at[j], {"dp": sib})

    def send_b(j):
        here = wfull.at[across, span(other_g, j)]
        return remote(here, here, sbs.at[j], sbr.at[j], {"dp": sib})

    def got_b(j):
        here = wfull.at[diag, span(other_g, j)]
        return remote(here, here, sbs.at[j], sbr.at[j], {"dp": sib})

    send_own = remote(w_ref, wfull.at[d], own_s, own_r, {"dp": sib})
    got_own = remote(w_ref, wfull.at[sib], own_s, own_r, {"dp": sib})

    def up_copy(i):
        block = c - i
        src = og_ref if i == 0 else oall.at[block]
        return remote(src, oall.at[block], os_.at[0, i], or_.at[0, i], {"corpus": c + 1})

    def up_got(i):
        here = oall.at[c - 1 - i]
        return remote(here, here, os_.at[0, i], or_.at[0, i], {"corpus": c - 1})

    def down_copy(i):
        block = c + i
        src = og_ref if i == 0 else oall.at[block]
        return remote(src, oall.at[block], os_.at[1, i], or_.at[1, i], {"corpus": c - 1})

    def down_got(i):
        here = oall.at[c + 1 + i]
        return remote(here, here, os_.at[1, i], or_.at[1, i], {"corpus": c + 1})

    for j in range(pieces):
        send_x(j).start()

    def line_step(i):
        if i > 0:
            @pl.when(c - i >= 0)
            def _():
                up_got(i - 1).wait_recv()

            @pl.when(c + i <= last)
            def _():
                down_got(i - 1).wait_recv()

        if i < last:
            @pl.when((c - i >= 0) & (c < last))
            def _():
                up_copy(i).start()

            @pl.when((c + i <= last) & (c > 0))
            def _():
                down_copy(i).start()

    line_step(0)
    for load in loads:
        load.start()
    send_own.start()
    loads[4].wait()
    rank = pin_ref.shape[0]
    out_ref[:, :rank] = lax.dot_general(
        hid_v[...], pin_ref[...], NT, preferred_element_type=jnp.float32
    )

    right_ref[...] = jnp.zeros_like(right_ref)
    per_unit = UNIT // PIECE
    units = 2 * (half // UNIT)

    def compute(n):
        side = g + lax.rem(n, 2) * (1 - 2 * g)
        here = pl.ds(pl.multiple_of(side * half + (n // 2) * UNIT, UNIT), UNIT)
        total = lax.dot_general(oall[0], wfull[0, here, :], NT, preferred_element_type=jnp.float32)
        for s in range(1, corpus_count):
            total += lax.dot_general(
                oall[s], wfull[s, here, :], NT, preferred_element_type=jnp.float32
            )
        value = gate_v[:, here].astype(jnp.float32)
        sig = 1.0 / (1.0 + jnp.exp(-value))
        grad = total * up_v[:, here].astype(jnp.float32) * sig * (1.0 + value * (1.0 - sig))
        right_ref[...] += lax.dot_general(
            grad.astype(jnp.bfloat16), pout_ref[:, here], NT, preferred_element_type=jnp.float32
        )

    done = 0

    def advance(upto):
        nonlocal done
        upto = min(upto, units)
        if upto <= done:
            return
        if done == 0:
            for load in loads[:4]:
                load.wait()
            got_own.wait_recv()
        for n in range(done, upto):
            got = got_a if n % 2 == 0 else got_b
            for k in range(per_unit):
                got((n // 2) * per_unit + k).wait_recv()

        @pl.loop(done, upto)
        def _(n):
            compute(n)

        done = upto

    step = 1
    for j in range(pieces):
        got_x(j).wait_recv()
        send_y(j).start()
        send_a(j).start()
        if j > 0:
            got_y(j - 1).wait_recv()
            send_b(j - 1).start()
        if j == 4 * step - 1 and step <= last:
            line_step(step)
            step += 1
        if step > last:
            advance(min(4 * (j - 4 * last + 2), 2 * (j // per_unit) - 1))
    while step <= last:
        line_step(step)
        step += 1
    got_y(pieces - 1).wait_recv()
    send_b(pieces - 1).start()
    advance(units - 1)
    advance(units)

    out_ref[:, rank:] = right_ref[...]
    send_own.wait_send()
    for j in range(pieces):
        send_x(j).wait_send()
        send_y(j).wait_send()
        send_a(j).wait_send()
        send_b(j).wait_send()
    for i in range(last):
        @pl.when((c - i >= 0) & (c < last))
        def _():
            up_copy(i).wait_send()

        @pl.when((c + i <= last) & (c > 0))
        def _():
            down_copy(i).wait_send()


def fused_parts(corpus_count, hidden_in, gate_pre, up_out, out_grad, w_down, proj_in, proj_out):
    tokens, depth = out_grad.shape
    rows = w_down.shape[0]
    rank = proj_in.shape[1]
    pieces = rows // 2 // PIECE
    dma = pltpu.SemaphoreType.DMA
    anywhere = pl.BlockSpec(memory_space=pl.ANY)
    inside = pl.BlockSpec(memory_space=pltpu.VMEM)
    return pl.pallas_call(
        functools.partial(fused_kernel, corpus_count),
        out_shape=jax.ShapeDtypeStruct((tokens, 2 * rank), jnp.float32),
        in_specs=[anywhere] * 5 + [inside] * 2,
        out_specs=inside,
        scratch_shapes=[
            pltpu.VMEM((tokens, rank), jnp.float32),
            pltpu.VMEM((4, rows, depth), jnp.bfloat16),
            pltpu.VMEM((corpus_count, tokens, depth), jnp.bfloat16),
            pltpu.VMEM((tokens, rows), jnp.bfloat16),
            pltpu.VMEM((tokens, rows), jnp.bfloat16),
            pltpu.VMEM(hidden_in.shape, jnp.bfloat16),
            dma((5,)), dma, dma,
        ]
        + [dma((pieces,))] * 8
        + [dma((2, corpus_count)), dma((2, corpus_count))],
        compiler_params=pltpu.CompilerParams(
            collective_id=0, has_side_effects=True, vmem_limit_bytes=56 * 1024 * 1024
        ),
    )(hidden_in, gate_pre, up_out, out_grad, w_down, proj_in.T, proj_out.T)


def tail_kernel(
    corpus_count, dp_count,
    lr_ref, lengths_ref, slab_ref,
    grads_ref, means_ref,
    box1, box2, box3, box4, rows_out,
    s1, r1, s2, r2, s3, r3, s4, r4,
):
    c = lax.axis_index("corpus")
    d = lax.axis_index("dp")
    tokens = lr_ref.shape[0]
    rank = lr_ref.shape[1] // 2
    share = tokens // corpus_count
    per_prompt = LENGTH // share
    prompts = tokens // LENGTH
    mesh_id = pl.DeviceIdType.MESH
    hops = range(1, corpus_count)
    dp_hops = range(1, dp_count)
    everyone = [(i, j) for i in range(corpus_count) for j in range(dp_count) if (i, j) != (0, 0)]

    def c_of(hop):
        return lax.rem(c + hop, corpus_count)

    def d_of(hop):
        return lax.rem(d + hop, dp_count)

    barrier = pltpu.get_barrier_semaphore()
    for i, j in everyone:
        pl.semaphore_signal(
            barrier, inc=1, device_id={"corpus": c_of(i), "dp": d_of(j)}, device_id_type=mesh_id
        )
    pl.semaphore_wait(barrier, len(everyone))

    def remote(src, dst, ssem, rsem, where):
        return pltpu.make_async_remote_copy(
            src_ref=src, dst_ref=dst, send_sem=ssem, recv_sem=rsem,
            device_id=where, device_id_type=mesh_id,
        )

    def part_of(who):
        return lr_ref.at[pl.ds(pl.multiple_of(who * share, share), share)]

    sent = []

    def send(*args):
        copy = remote(*args)
        copy.start()
        sent.append(copy)

    for hop in hops:
        send(part_of(c_of(hop)), box1.at[c], s1.at[hop], r1.at[c], {"corpus": c_of(hop)})
    total = lr_ref[pl.ds(pl.multiple_of(c * share, share), share), :]
    for hop in hops:
        who = c_of(hop)
        remote(box1.at[who], box1.at[who], s1.at[hop], r1.at[who], {"corpus": who}).wait_recv()
        total += box1[who]

    position = lax.rem(c, per_prompt) * share + lax.broadcasted_iota(jnp.int32, (share, rank), 0)
    used = position < lengths_ref[c // per_prompt]
    left = jnp.where(used, total[:, :rank], 0.0)
    box2[c] = lax.dot_general(
        left, total[:, rank:], (((0,), (0,)), ((), ())),
        precision=lax.Precision.HIGHEST, preferred_element_type=jnp.float32,
    )
    for hop in hops:
        send(box2.at[c], box2.at[c], s2.at[hop], r2.at[c], {"corpus": c_of(hop)})
    for hop in hops:
        who = c_of(hop)
        remote(box2.at[who], box2.at[who], s2.at[hop], r2.at[who], {"corpus": who}).wait_recv()

    for q in range(prompts):
        whole = box2[q * per_prompt]
        for k in range(1, per_prompt):
            whole += box2[q * per_prompt + k]
        for r in range(rank):
            grads_ref[q : q + 1, r * rank : (r + 1) * rank] = whole[r : r + 1, :]

    box3[d] = grads_ref[...]
    for hop in dp_hops:
        send(box3.at[d], box3.at[d], s3.at[hop], r3.at[d], {"dp": d_of(hop)})
    for hop in dp_hops:
        who = d_of(hop)
        remote(box3.at[who], box3.at[who], s3.at[hop], r3.at[who], {"dp": who}).wait_recv()
    queries = jnp.concatenate([box3[k] for k in range(dp_count)], axis=0).astype(jnp.bfloat16)
    scores = lax.dot_general(queries, slab_ref[...], NT, preferred_element_type=jnp.float32)
    scores = scores * (4.0 / math.sqrt(GRAD * LENGTH))
    for k in range(dp_count):
        rows_out[k] = scores[k * prompts : (k + 1) * prompts, :]

    slot = c * dp_count + d
    box4[slot] = rows_out[d]
    for n, (i, j) in enumerate(everyone):
        send(
            rows_out.at[d_of(j)], box4.at[slot], s4.at[n], r4.at[slot],
            {"corpus": c_of(i), "dp": d_of(j)},
        )
    for n, (i, j) in enumerate(everyone):
        other = c_of(i) * dp_count + d_of(j)
        here = box4.at[other]
        remote(here, here, s4.at[n], r4.at[other], {"corpus": c_of(i), "dp": d_of(j)}).wait_recv()

    values = jnp.concatenate([box4[k] for k in range(corpus_count * dp_count)], axis=1)
    top = jnp.max(values, axis=1, keepdims=True)
    taken = jnp.zeros((prompts, 1), jnp.float32)
    total = jnp.zeros((prompts, 1), jnp.float32)
    for n in range(TOPK):
        count = jnp.sum((values == top).astype(jnp.float32), axis=1, keepdims=True)
        use = jnp.minimum(count, TOPK - taken)
        total += use * top
        taken += use
        if n < TOPK - 1:
            top = jnp.max(jnp.where(values < top, values, -3e38), axis=1, keepdims=True)
    means_ref[...] = jnp.broadcast_to(total * (1.0 / TOPK), means_ref.shape)
    for copy in sent:
        copy.wait_send()


def fused_tail(corpus_count, dp_count, left_right, lengths, slab):
    tokens, width = left_right.shape
    rank = width // 2
    prompts = lengths.shape[0]
    examples = slab.shape[0]
    dma = pltpu.SemaphoreType.DMA
    everyone = corpus_count * dp_count
    inside = pl.BlockSpec(memory_space=pltpu.VMEM)
    f32 = jnp.float32
    grads, means = pl.pallas_call(
        functools.partial(tail_kernel, corpus_count, dp_count),
        out_shape=(
            jax.ShapeDtypeStruct((prompts, GRAD), f32),
            jax.ShapeDtypeStruct((prompts, 128), f32),
        ),
        in_specs=[inside, pl.BlockSpec(memory_space=pltpu.SMEM), inside],
        out_specs=(inside, inside),
        scratch_shapes=[
            pltpu.VMEM((corpus_count, tokens // corpus_count, width), f32),
            pltpu.VMEM((corpus_count, rank, rank), f32),
            pltpu.VMEM((dp_count, prompts, GRAD), f32),
            pltpu.VMEM((everyone, prompts, examples), f32),
            pltpu.VMEM((dp_count, prompts, examples), f32),
            dma((corpus_count,)), dma((corpus_count,)),
            dma((corpus_count,)), dma((corpus_count,)),
            dma((dp_count,)), dma((dp_count,)),
            dma((everyone,)), dma((everyone,)),
        ],
        compiler_params=pltpu.CompilerParams(
            collective_id=1, has_side_effects=True, vmem_limit_bytes=16 * 1024 * 1024
        ),
    )(left_right, lengths, slab)
    return grads, means[:, 0]


def plain_parts(hidden_in, gate_pre, up_out, out_grad, w_down, proj_in, proj_out):
    full_weight = lax.all_gather(w_down, "dp", axis=1, tiled=True)
    grad_hidden = lax.dot_general(
        lax.all_gather(out_grad, "corpus", axis=1, tiled=True),
        full_weight,
        NT,
        preferred_element_type=jnp.float32,
    )
    gate_value = gate_pre.astype(jnp.float32)
    sigmoid_gate = jax.nn.sigmoid(gate_value)
    gate_grad = (
        grad_hidden
        * up_out.astype(jnp.float32)
        * sigmoid_gate
        * (1.0 + gate_value * (1.0 - sigmoid_gate))
    ).astype(jnp.bfloat16)
    left_part = jnp.dot(hidden_in, proj_in, preferred_element_type=jnp.float32)
    right_part = jnp.dot(gate_grad, proj_out, preferred_element_type=jnp.float32)
    return left_part, right_part


def local(fused, corpus_count, hidden_in, gate_pre, up_out, out_grad, w_down, proj_in, proj_out, lengths, slab):
    tok_rows = hidden_in.shape[0]
    query_count = lengths.shape[0]
    layer = (hidden_in, gate_pre, up_out, out_grad, w_down, proj_in, proj_out)
    if fused:
        left_right = fused_parts(corpus_count, *layer)
        return fused_tail(corpus_count, 4, left_right, lengths, slab)
    left_part, right_part = plain_parts(*layer)
    token_index = jnp.arange(tok_rows, dtype=jnp.int32)
    position = token_index % LENGTH
    prompt_of = token_index // LENGTH
    prompt_ids = jnp.arange(query_count, dtype=jnp.int32)
    mask_table = (
        (prompt_of[:, None] == prompt_ids[None, :]) & (position[:, None] < lengths[None, :])
    ).astype(jnp.float32)
    left_all, right_all = lax.psum((left_part, right_part), "corpus")
    example_grads = jnp.einsum(
        "tq,tr,tc->qrc", mask_table, left_all, right_all, precision=lax.Precision.HIGHEST
    )
    query_grads = example_grads.reshape(query_count, GRAD)
    queries = lax.all_gather(query_grads.astype(jnp.bfloat16), "dp", axis=0, tiled=True)
    scores = lax.dot_general(queries, slab, NT, preferred_element_type=jnp.float32)
    scores = scores * (4.0 / math.sqrt(GRAD * LENGTH))
    leaders = lax.top_k(scores, TOPK)[0]
    gathered = lax.all_gather(leaders, ("corpus", "dp"), axis=1, tiled=True)
    leaders = lax.top_k(gathered, TOPK)[0]
    own_rows = lax.dynamic_slice_in_dim(leaders, lax.axis_index("dp") * query_count, query_count, 0)
    return (query_grads, jnp.mean(own_rows, axis=1))


def solution(mesh):
    sizes = dict(mesh.shape)
    fused = sizes["groups"] == 2 and sizes["dp"] == 4 and sizes["corpus"] == 4
    in_specs = (
        P(("groups", "dp"), "corpus"),
        P(("groups", "dp"), "corpus"),
        P(("groups", "dp"), "corpus"),
        P(("groups", "dp"), "corpus"),
        P("corpus", "dp"),
        P("corpus", None),
        P("corpus", None),
        P(("groups", "dp")),
        P(("groups", "corpus", "dp"), None),
    )
    out_specs = (P(("groups", "dp"), None), P(("groups", "dp")))
    return jax.shard_map(
        functools.partial(local, fused, sizes["corpus"]),
        mesh=mesh, in_specs=in_specs, out_specs=out_specs, check_vma=False,
    )
```

```python
import functools
import math

import jax
import jax.numpy as jnp
from jax import lax
from jax.experimental import pallas as pl
from jax.experimental.pallas import tpu as pltpu
from jax.sharding import PartitionSpec as P

TOPK = 16
LENGTH = 256
GRAD = 4096
PIECE = 128
UNIT = 256
NT = (((1,), (1,)), ((), ()))


def fused_kernel(
    corpus_count,
    hidden_ref, gate_ref, up_ref, og_ref, w_ref, pin_ref, pout_ref,
    out_ref,
    right_ref, wfull, oall, gate_v, up_v, hid_v,
    local_sem, own_s, own_r, xs, xr, ys, yr, sas, sar, sbs, sbr, os_, or_,
):
    g = lax.axis_index("groups")
    c = lax.axis_index("corpus")
    d = lax.axis_index("dp")
    other_g = 1 - g
    sib = d + 1 - 2 * lax.rem(d, 2)
    across = lax.rem(d + 2, 4)
    diag = lax.rem(sib + 2, 4)
    rows = w_ref.shape[0]
    half = rows // 2
    pieces = half // PIECE
    last = corpus_count - 1

    barrier = pltpu.get_barrier_semaphore()

    def greet(where):
        pl.semaphore_signal(
            barrier, inc=1, device_id=where, device_id_type=pl.DeviceIdType.MESH
        )

    greet({"dp": sib})
    greet({"dp": across})
    greet({"groups": other_g})

    for hop in range(1, corpus_count):
        greet({"corpus": lax.rem(c + hop, corpus_count)})

    loads = [
        pltpu.make_async_copy(w_ref, wfull.at[d], local_sem.at[0]),
        pltpu.make_async_copy(og_ref, oall.at[c], local_sem.at[1]),
        pltpu.make_async_copy(gate_ref, gate_v, local_sem.at[2]),
        pltpu.make_async_copy(up_ref, up_v, local_sem.at[3]),
        pltpu.make_async_copy(hidden_ref, hid_v, local_sem.at[4]),
    ]
    pl.semaphore_wait(barrier, 2 + corpus_count)

    def remote(src, dst, ssem, rsem, where):
        return pltpu.make_async_remote_copy(
            src_ref=src, dst_ref=dst, send_sem=ssem, recv_sem=rsem,
            device_id=where, device_id_type=pl.DeviceIdType.MESH,
        )

    def span(side, j):
        return pl.ds(pl.multiple_of(side * half + j * PIECE, PIECE), PIECE)

    def send_x(j):
        return remote(w_ref.at[span(g, j)], wfull.at[d, span(g, j)], xs.at[j], xr.at[j], {"dp": across})

    def got_x(j):
        here = wfull.at[across, span(g, j)]
        return remote(here, here, xs.at[j], xr.at[j], {"dp": across})

    def send_y(j):
        here = wfull.at[across, span(g, j)]
        return remote(here, here, ys.at[j], yr.at[j], {"groups": other_g})

    def got_y(j):
        here = wfull.at[across, span(other_g, j)]
        return remote(here, here, ys.at[j], yr.at[j], {"groups": other_g})

    def send_a(j):
        here = wfull.at[across, span(g, j)]
        return remote(here, here, sas.at[j], sar.at[j], {"dp": sib})

    def got_a(j):
        here = wfull.at[diag, span(g, j)]
        return remote(here, here, sas.at[j], sar.at[j], {"dp": sib})

    def send_b(j):
        here = wfull.at[across, span(other_g, j)]
        return remote(here, here, sbs.at[j], sbr.at[j], {"dp": sib})

    def got_b(j):
        here = wfull.at[diag, span(other_g, j)]
        return remote(here, here, sbs.at[j], sbr.at[j], {"dp": sib})

    send_own = remote(w_ref, wfull.at[d], own_s, own_r, {"dp": sib})
    got_own = remote(w_ref, wfull.at[sib], own_s, own_r, {"dp": sib})

    def up_copy(i):
        block = c - i
        src = og_ref if i == 0 else oall.at[block]
        return remote(src, oall.at[block], os_.at[0, i], or_.at[0, i], {"corpus": c + 1})

    def up_got(i):
        here = oall.at[c - 1 - i]
        return remote(here, here, os_.at[0, i], or_.at[0, i], {"corpus": c - 1})

    def down_copy(i):
        block = c + i
        src = og_ref if i == 0 else oall.at[block]
        return remote(src, oall.at[block], os_.at[1, i], or_.at[1, i], {"corpus": c - 1})

    def down_got(i):
        here = oall.at[c + 1 + i]
        return remote(here, here, os_.at[1, i], or_.at[1, i], {"corpus": c + 1})

    for j in range(pieces):
        send_x(j).start()

    def line_step(i):
        if i > 0:
            @pl.when(c - i >= 0)
            def _():
                up_got(i - 1).wait_recv()

            @pl.when(c + i <= last)
            def _():
                down_got(i - 1).wait_recv()

        if i < last:
            @pl.when((c - i >= 0) & (c < last))
            def _():
                up_copy(i).start()

            @pl.when((c + i <= last) & (c > 0))
            def _():
                down_copy(i).start()

    line_step(0)
    for load in loads:
        load.start()
    send_own.start()
    loads[4].wait()
    rank = pin_ref.shape[0]
    out_ref[:, :rank] = lax.dot_general(
        hid_v[...], pin_ref[...], NT, preferred_element_type=jnp.float32
    )

    right_ref[...] = jnp.zeros_like(right_ref)
    per_unit = UNIT // PIECE
    units = 2 * (half // UNIT)

    def compute(n):
        side = g + lax.rem(n, 2) * (1 - 2 * g)
        here = pl.ds(pl.multiple_of(side * half + (n // 2) * UNIT, UNIT), UNIT)
        total = lax.dot_general(oall[0], wfull[0, here, :], NT, preferred_element_type=jnp.float32)
        for s in range(1, corpus_count):
            total += lax.dot_general(
                oall[s], wfull[s, here, :], NT, preferred_element_type=jnp.float32
            )
        value = gate_v[:, here].astype(jnp.float32)
        sig = 1.0 / (1.0 + jnp.exp(-value))
        grad = total * up_v[:, here].astype(jnp.float32) * sig * (1.0 + value * (1.0 - sig))
        right_ref[...] += lax.dot_general(
            grad.astype(jnp.bfloat16), pout_ref[:, here], NT, preferred_element_type=jnp.float32
        )

    done = 0

    def advance(upto):
        nonlocal done
        upto = min(upto, units)
        if upto <= done:
            return
        if done == 0:
            for load in loads[:4]:
                load.wait()
            got_own.wait_recv()
        for n in range(done, upto):
            got = got_a if n % 2 == 0 else got_b
            for k in range(per_unit):
                got((n // 2) * per_unit + k).wait_recv()

        @pl.loop(done, upto)
        def _(n):
            compute(n)

        done = upto

    step = 1
    for j in range(pieces):
        got_x(j).wait_recv()
        send_y(j).start()
        send_a(j).start()
        if j > 0:
            got_y(j - 1).wait_recv()
            send_b(j - 1).start()
        if j == 4 * step - 1 and step <= last:
            line_step(step)
            step += 1
        if step > last:
            advance(min(4 * (j - 4 * last + 2), 2 * (j // per_unit)))
    while step <= last:
        line_step(step)
        step += 1
    got_y(pieces - 1).wait_recv()
    send_b(pieces - 1).start()
    advance(units - 1)
    advance(units)

    out_ref[:, rank:] = right_ref[...]
    send_own.wait_send()
    for j in range(pieces):
        send_x(j).wait_send()
        send_y(j).wait_send()
        send_a(j).wait_send()
        send_b(j).wait_send()
    for i in range(last):
        @pl.when((c - i >= 0) & (c < last))
        def _():
            up_copy(i).wait_send()

        @pl.when((c + i <= last) & (c > 0))
        def _():
            down_copy(i).wait_send()


def fused_parts(corpus_count, hidden_in, gate_pre, up_out, out_grad, w_down, proj_in, proj_out):
    tokens, depth = out_grad.shape
    rows = w_down.shape[0]
    rank = proj_in.shape[1]
    pieces = rows // 2 // PIECE
    dma = pltpu.SemaphoreType.DMA
    anywhere = pl.BlockSpec(memory_space=pl.ANY)
    inside = pl.BlockSpec(memory_space=pltpu.VMEM)
    return pl.pallas_call(
        functools.partial(fused_kernel, corpus_count),
        out_shape=jax.ShapeDtypeStruct((tokens, 2 * rank), jnp.float32),
        in_specs=[anywhere] * 5 + [inside] * 2,
        out_specs=inside,
        scratch_shapes=[
            pltpu.VMEM((tokens, rank), jnp.float32),
            pltpu.VMEM((4, rows, depth), jnp.bfloat16),
            pltpu.VMEM((corpus_count, tokens, depth), jnp.bfloat16),
            pltpu.VMEM((tokens, rows), jnp.bfloat16),
            pltpu.VMEM((tokens, rows), jnp.bfloat16),
            pltpu.VMEM(hidden_in.shape, jnp.bfloat16),
            dma((5,)), dma, dma,
        ]
        + [dma((pieces,))] * 8
        + [dma((2, corpus_count)), dma((2, corpus_count))],
        compiler_params=pltpu.CompilerParams(
            collective_id=0, has_side_effects=True, vmem_limit_bytes=56 * 1024 * 1024
        ),
    )(hidden_in, gate_pre, up_out, out_grad, w_down, proj_in.T, proj_out.T)


def tail_kernel(
    corpus_count, dp_count,
    lr_ref, lengths_ref, slab_ref,
    grads_ref, means_ref,
    box1, box2, box3, box4, rows_out,
    s1, r1, s2, r2, s3, r3, s4, r4,
):
    c = lax.axis_index("corpus")
    d = lax.axis_index("dp")
    tokens = lr_ref.shape[0]
    rank = lr_ref.shape[1] // 2
    share = tokens // corpus_count
    per_prompt = LENGTH // share
    prompts = tokens // LENGTH
    mesh_id = pl.DeviceIdType.MESH
    hops = range(1, corpus_count)
    dp_hops = range(1, dp_count)
    everyone = [(i, j) for i in range(corpus_count) for j in range(dp_count) if (i, j) != (0, 0)]

    def c_of(hop):
        return lax.rem(c + hop, corpus_count)

    def d_of(hop):
        return lax.rem(d + hop, dp_count)

    barrier = pltpu.get_barrier_semaphore()
    for i, j in everyone:
        pl.semaphore_signal(
            barrier, inc=1, device_id={"corpus": c_of(i), "dp": d_of(j)}, device_id_type=mesh_id
        )
    pl.semaphore_wait(barrier, len(everyone))

    def remote(src, dst, ssem, rsem, where):
        return pltpu.make_async_remote_copy(
            src_ref=src, dst_ref=dst, send_sem=ssem, recv_sem=rsem,
            device_id=where, device_id_type=mesh_id,
        )

    def part_of(who):
        return lr_ref.at[pl.ds(pl.multiple_of(who * share, share), share)]

    sent = []

    def send(*args):
        copy = remote(*args)
        copy.start()
        sent.append(copy)

    for hop in hops:
        send(part_of(c_of(hop)), box1.at[c], s1.at[hop], r1.at[c], {"corpus": c_of(hop)})
    total = lr_ref[pl.ds(pl.multiple_of(c * share, share), share), :]
    for hop in hops:
        who = c_of(hop)
        remote(box1.at[who], box1.at[who], s1.at[hop], r1.at[who], {"corpus": who}).wait_recv()
        total += box1[who]

    position = lax.rem(c, per_prompt) * share + lax.broadcasted_iota(jnp.int32, (share, rank), 0)
    used = position < lengths_ref[c // per_prompt]
    left = jnp.where(used, total[:, :rank], 0.0)
    box2[c] = lax.dot_general(
        left, total[:, rank:], (((0,), (0,)), ((), ())),
        precision=lax.Precision.HIGHEST, preferred_element_type=jnp.float32,
    )
    for hop in hops:
        send(box2.at[c], box2.at[c], s2.at[hop], r2.at[c], {"corpus": c_of(hop)})
    for hop in hops:
        who = c_of(hop)
        remote(box2.at[who], box2.at[who], s2.at[hop], r2.at[who], {"corpus": who}).wait_recv()

    for q in range(prompts):
        whole = box2[q * per_prompt]
        for k in range(1, per_prompt):
            whole += box2[q * per_prompt + k]
        for r in range(rank):
            grads_ref[q : q + 1, r * rank : (r + 1) * rank] = whole[r : r + 1, :]

    box3[d] = grads_ref[...]
    for hop in dp_hops:
        send(box3.at[d], box3.at[d], s3.at[hop], r3.at[d], {"dp": d_of(hop)})
    for hop in dp_hops:
        who = d_of(hop)
        remote(box3.at[who], box3.at[who], s3.at[hop], r3.at[who], {"dp": who}).wait_recv()
    queries = jnp.concatenate([box3[k] for k in range(dp_count)], axis=0).astype(jnp.bfloat16)
    scores = lax.dot_general(queries, slab_ref[...], NT, preferred_element_type=jnp.float32)
    scores = scores * (4.0 / math.sqrt(GRAD * LENGTH))
    for k in range(dp_count):
        rows_out[k] = scores[k * prompts : (k + 1) * prompts, :]

    slot = c * dp_count + d
    box4[slot] = rows_out[d]
    for n, (i, j) in enumerate(everyone):
        send(
            rows_out.at[d_of(j)], box4.at[slot], s4.at[n], r4.at[slot],
            {"corpus": c_of(i), "dp": d_of(j)},
        )
    for n, (i, j) in enumerate(everyone):
        other = c_of(i) * dp_count + d_of(j)
        here = box4.at[other]
        remote(here, here, s4.at[n], r4.at[other], {"corpus": c_of(i), "dp": d_of(j)}).wait_recv()

    values = jnp.concatenate([box4[k] for k in range(corpus_count * dp_count)], axis=1)
    top = jnp.max(values, axis=1, keepdims=True)
    taken = jnp.zeros((prompts, 1), jnp.float32)
    total = jnp.zeros((prompts, 1), jnp.float32)
    for n in range(TOPK):
        count = jnp.sum((values == top).astype(jnp.float32), axis=1, keepdims=True)
        use = jnp.minimum(count, TOPK - taken)
        total += use * top
        taken += use
        if n < TOPK - 1:
            top = jnp.max(jnp.where(values < top, values, -3e38), axis=1, keepdims=True)
    means_ref[...] = jnp.broadcast_to(total * (1.0 / TOPK), means_ref.shape)
    for copy in sent:
        copy.wait_send()


def fused_tail(corpus_count, dp_count, left_right, lengths, slab):
    tokens, width = left_right.shape
    rank = width // 2
    prompts = lengths.shape[0]
    examples = slab.shape[0]
    dma = pltpu.SemaphoreType.DMA
    everyone = corpus_count * dp_count
    inside = pl.BlockSpec(memory_space=pltpu.VMEM)
    f32 = jnp.float32
    grads, means = pl.pallas_call(
        functools.partial(tail_kernel, corpus_count, dp_count),
        out_shape=(
            jax.ShapeDtypeStruct((prompts, GRAD), f32),
            jax.ShapeDtypeStruct((prompts, 128), f32),
        ),
        in_specs=[inside, pl.BlockSpec(memory_space=pltpu.SMEM), inside],
        out_specs=(inside, inside),
        scratch_shapes=[
            pltpu.VMEM((corpus_count, tokens // corpus_count, width), f32),
            pltpu.VMEM((corpus_count, rank, rank), f32),
            pltpu.VMEM((dp_count, prompts, GRAD), f32),
            pltpu.VMEM((everyone, prompts, examples), f32),
            pltpu.VMEM((dp_count, prompts, examples), f32),
            dma((corpus_count,)), dma((corpus_count,)),
            dma((corpus_count,)), dma((corpus_count,)),
            dma((dp_count,)), dma((dp_count,)),
            dma((everyone,)), dma((everyone,)),
        ],
        compiler_params=pltpu.CompilerParams(
            collective_id=1, has_side_effects=True, vmem_limit_bytes=16 * 1024 * 1024
        ),
    )(left_right, lengths, slab)
    return grads, means[:, 0]


def plain_parts(hidden_in, gate_pre, up_out, out_grad, w_down, proj_in, proj_out):
    full_weight = lax.all_gather(w_down, "dp", axis=1, tiled=True)
    grad_hidden = lax.dot_general(
        lax.all_gather(out_grad, "corpus", axis=1, tiled=True),
        full_weight,
        NT,
        preferred_element_type=jnp.float32,
    )
    gate_value = gate_pre.astype(jnp.float32)
    sigmoid_gate = jax.nn.sigmoid(gate_value)
    gate_grad = (
        grad_hidden
        * up_out.astype(jnp.float32)
        * sigmoid_gate
        * (1.0 + gate_value * (1.0 - sigmoid_gate))
    ).astype(jnp.bfloat16)
    left_part = jnp.dot(hidden_in, proj_in, preferred_element_type=jnp.float32)
    right_part = jnp.dot(gate_grad, proj_out, preferred_element_type=jnp.float32)
    return left_part, right_part


def local(fused, corpus_count, hidden_in, gate_pre, up_out, out_grad, w_down, proj_in, proj_out, lengths, slab):
    tok_rows = hidden_in.shape[0]
    query_count = lengths.shape[0]
    layer = (hidden_in, gate_pre, up_out, out_grad, w_down, proj_in, proj_out)
    if fused:
        left_right = fused_parts(corpus_count, *layer)
        return fused_tail(corpus_count, 4, left_right, lengths, slab)
    left_part, right_part = plain_parts(*layer)
    token_index = jnp.arange(tok_rows, dtype=jnp.int32)
    position = token_index % LENGTH
    prompt_of = token_index // LENGTH
    prompt_ids = jnp.arange(query_count, dtype=jnp.int32)
    mask_table = (
        (prompt_of[:, None] == prompt_ids[None, :]) & (position[:, None] < lengths[None, :])
    ).astype(jnp.float32)
    left_all, right_all = lax.psum((left_part, right_part), "corpus")
    example_grads = jnp.einsum(
        "tq,tr,tc->qrc", mask_table, left_all, right_all, precision=lax.Precision.HIGHEST
    )
    query_grads = example_grads.reshape(query_count, GRAD)
    queries = lax.all_gather(query_grads.astype(jnp.bfloat16), "dp", axis=0, tiled=True)
    scores = lax.dot_general(queries, slab, NT, preferred_element_type=jnp.float32)
    scores = scores * (4.0 / math.sqrt(GRAD * LENGTH))
    leaders = lax.top_k(scores, TOPK)[0]
    gathered = lax.all_gather(leaders, ("corpus", "dp"), axis=1, tiled=True)
    leaders = lax.top_k(gathered, TOPK)[0]
    own_rows = lax.dynamic_slice_in_dim(leaders, lax.axis_index("dp") * query_count, query_count, 0)
    return (query_grads, jnp.mean(own_rows, axis=1))


def solution(mesh):
    sizes = dict(mesh.shape)
    fused = sizes["groups"] == 2 and sizes["dp"] == 4 and sizes["corpus"] == 4
    in_specs = (
        P(("groups", "dp"), "corpus"),
        P(("groups", "dp"), "corpus"),
        P(("groups", "dp"), "corpus"),
        P(("groups", "dp"), "corpus"),
        P("corpus", "dp"),
        P("corpus", None),
        P("corpus", None),
        P(("groups", "dp")),
        P(("groups", "corpus", "dp"), None),
    )
    out_specs = (P(("groups", "dp"), None), P(("groups", "dp")))
    return jax.shard_map(
        functools.partial(local, fused, sizes["corpus"]),
        mesh=mesh, in_specs=in_specs, out_specs=out_specs, check_vma=False,
    )
```

```python
import functools
import math

import jax
import jax.numpy as jnp
from jax import lax
from jax.experimental import pallas as pl
from jax.experimental.pallas import tpu as pltpu
from jax.sharding import PartitionSpec as P

TOPK = 16
LENGTH = 256
GRAD = 4096
PIECE = 128
UNIT = 256
NT = (((1,), (1,)), ((), ()))


def fused_kernel(
    corpus_count,
    hidden_ref, gate_ref, up_ref, og_ref, w_ref, pin_ref, pout_ref,
    out_ref,
    right_ref, wfull, oall, gate_v, up_v, hid_v,
    local_sem, own_s, own_r, xs, xr, ys, yr, sas, sar, sbs, sbr, os_, or_,
):
    g = lax.axis_index("groups")
    c = lax.axis_index("corpus")
    d = lax.axis_index("dp")
    other_g = 1 - g
    sib = d + 1 - 2 * lax.rem(d, 2)
    across = lax.rem(d + 2, 4)
    diag = lax.rem(sib + 2, 4)
    rows = w_ref.shape[0]
    half = rows // 2
    pieces = half // PIECE
    last = corpus_count - 1

    barrier = pltpu.get_barrier_semaphore()

    def greet(where):
        pl.semaphore_signal(
            barrier, inc=1, device_id=where, device_id_type=pl.DeviceIdType.MESH
        )

    greet({"dp": sib})
    greet({"dp": across})
    greet({"groups": other_g})

    for hop in range(1, corpus_count):
        greet({"corpus": lax.rem(c + hop, corpus_count)})

    loads = [
        pltpu.make_async_copy(w_ref, wfull.at[d], local_sem.at[0]),
        pltpu.make_async_copy(og_ref, oall.at[c], local_sem.at[1]),
        pltpu.make_async_copy(gate_ref, gate_v, local_sem.at[2]),
        pltpu.make_async_copy(up_ref, up_v, local_sem.at[3]),
        pltpu.make_async_copy(hidden_ref, hid_v, local_sem.at[4]),
    ]
    pl.semaphore_wait(barrier, 2 + corpus_count)

    def remote(src, dst, ssem, rsem, where):
        return pltpu.make_async_remote_copy(
            src_ref=src, dst_ref=dst, send_sem=ssem, recv_sem=rsem,
            device_id=where, device_id_type=pl.DeviceIdType.MESH,
        )

    def span(side, j):
        return pl.ds(pl.multiple_of(side * half + j * PIECE, PIECE), PIECE)

    def send_x(j):
        return remote(w_ref.at[span(g, j)], wfull.at[d, span(g, j)], xs.at[j], xr.at[j], {"dp": across})

    def got_x(j):
        here = wfull.at[across, span(g, j)]
        return remote(here, here, xs.at[j], xr.at[j], {"dp": across})

    def send_y(j):
        here = wfull.at[across, span(g, j)]
        return remote(here, here, ys.at[j], yr.at[j], {"groups": other_g})

    def got_y(j):
        here = wfull.at[across, span(other_g, j)]
        return remote(here, here, ys.at[j], yr.at[j], {"groups": other_g})

    def send_a(j):
        here = wfull.at[across, span(g, j)]
        return remote(here, here, sas.at[j], sar.at[j], {"dp": sib})

    def got_a(j):
        here = wfull.at[diag, span(g, j)]
        return remote(here, here, sas.at[j], sar.at[j], {"dp": sib})

    def send_b(j):
        here = wfull.at[across, span(other_g, j)]
        return remote(here, here, sbs.at[j], sbr.at[j], {"dp": sib})

    def got_b(j):
        here = wfull.at[diag, span(other_g, j)]
        return remote(here, here, sbs.at[j], sbr.at[j], {"dp": sib})

    send_own = remote(w_ref, wfull.at[d], own_s, own_r, {"dp": sib})
    got_own = remote(w_ref, wfull.at[sib], own_s, own_r, {"dp": sib})

    def up_copy(i):
        block = c - i
        src = og_ref if i == 0 else oall.at[block]
        return remote(src, oall.at[block], os_.at[0, i], or_.at[0, i], {"corpus": c + 1})

    def up_got(i):
        here = oall.at[c - 1 - i]
        return remote(here, here, os_.at[0, i], or_.at[0, i], {"corpus": c - 1})

    def down_copy(i):
        block = c + i
        src = og_ref if i == 0 else oall.at[block]
        return remote(src, oall.at[block], os_.at[1, i], or_.at[1, i], {"corpus": c - 1})

    def down_got(i):
        here = oall.at[c + 1 + i]
        return remote(here, here, os_.at[1, i], or_.at[1, i], {"corpus": c + 1})

    for j in range(pieces):
        send_x(j).start()

    def line_step(i):
        if i > 0:
            @pl.when(c - i >= 0)
            def _():
                up_got(i - 1).wait_recv()

            @pl.when(c + i <= last)
            def _():
                down_got(i - 1).wait_recv()

        if i < last:
            @pl.when((c - i >= 0) & (c < last))
            def _():
                up_copy(i).start()

            @pl.when((c + i <= last) & (c > 0))
            def _():
                down_copy(i).start()

    line_step(0)
    for load in loads:
        load.start()
    send_own.start()
    loads[4].wait()
    rank = pin_ref.shape[0]
    out_ref[:, :rank] = lax.dot_general(
        hid_v[...], pin_ref[...], NT, preferred_element_type=jnp.float32
    )

    right_ref[...] = jnp.zeros_like(right_ref)
    per_unit = UNIT // PIECE
    units = 2 * (half // UNIT)

    def compute(n):
        side = g + lax.rem(n, 2) * (1 - 2 * g)
        here = pl.ds(pl.multiple_of(side * half + (n // 2) * UNIT, UNIT), UNIT)
        total = lax.dot_general(oall[0], wfull[0, here, :], NT, preferred_element_type=jnp.float32)
        for s in range(1, corpus_count):
            total += lax.dot_general(
                oall[s], wfull[s, here, :], NT, preferred_element_type=jnp.float32
            )
        value = gate_v[:, here].astype(jnp.float32)
        sig = 1.0 / (1.0 + jnp.exp(-value))
        grad = total * up_v[:, here].astype(jnp.float32) * sig * (1.0 + value * (1.0 - sig))
        right_ref[...] += lax.dot_general(
            grad.astype(jnp.bfloat16), pout_ref[:, here], NT, preferred_element_type=jnp.float32
        )

    done = 0

    def advance(upto):
        nonlocal done
        upto = min(upto, units)
        if upto <= done:
            return
        if done == 0:
            for load in loads[:4]:
                load.wait()
            got_own.wait_recv()
        for n in range(done, upto):
            got = got_a if n % 2 == 0 else got_b
            for k in range(per_unit):
                got((n // 2) * per_unit + k).wait_recv()

        @pl.loop(done, upto)
        def _(n):
            compute(n)

        done = upto

    step = 1
    for j in range(pieces):
        got_x(j).wait_recv()
        send_y(j).start()
        send_a(j).start()
        if j > 0:
            got_y(j - 1).wait_recv()
            send_b(j - 1).start()
        if j == 4 * step - 1 and step <= last:
            line_step(step)
            step += 1
        if step > last:
            advance(min(4 * (j - 4 * last + 2), 2 * (j // per_unit) - 1))
    while step <= last:
        line_step(step)
        step += 1
    got_y(pieces - 1).wait_recv()
    send_b(pieces - 1).start()
    advance(units - 1)
    advance(units)

    out_ref[:, rank:] = right_ref[...]
    send_own.wait_send()
    for j in range(pieces):
        send_x(j).wait_send()
        send_y(j).wait_send()
        send_a(j).wait_send()
        send_b(j).wait_send()
    for i in range(last):
        @pl.when((c - i >= 0) & (c < last))
        def _():
            up_copy(i).wait_send()

        @pl.when((c + i <= last) & (c > 0))
        def _():
            down_copy(i).wait_send()


def fused_parts(corpus_count, hidden_in, gate_pre, up_out, out_grad, w_down, proj_in, proj_out):
    tokens, depth = out_grad.shape
    rows = w_down.shape[0]
    rank = proj_in.shape[1]
    pieces = rows // 2 // PIECE
    dma = pltpu.SemaphoreType.DMA
    anywhere = pl.BlockSpec(memory_space=pl.ANY)
    inside = pl.BlockSpec(memory_space=pltpu.VMEM)
    return pl.pallas_call(
        functools.partial(fused_kernel, corpus_count),
        out_shape=jax.ShapeDtypeStruct((tokens, 2 * rank), jnp.float32),
        in_specs=[anywhere] * 5 + [inside] * 2,
        out_specs=inside,
        scratch_shapes=[
            pltpu.VMEM((tokens, rank), jnp.float32),
            pltpu.VMEM((4, rows, depth), jnp.bfloat16),
            pltpu.VMEM((corpus_count, tokens, depth), jnp.bfloat16),
            pltpu.VMEM((tokens, rows), jnp.bfloat16),
            pltpu.VMEM((tokens, rows), jnp.bfloat16),
            pltpu.VMEM(hidden_in.shape, jnp.bfloat16),
            dma((5,)), dma, dma,
        ]
        + [dma((pieces,))] * 8
        + [dma((2, corpus_count)), dma((2, corpus_count))],
        compiler_params=pltpu.CompilerParams(
            collective_id=0, has_side_effects=True, vmem_limit_bytes=56 * 1024 * 1024
        ),
    )(hidden_in, gate_pre, up_out, out_grad, w_down, proj_in.T, proj_out.T)


def tail_kernel(
    corpus_count, dp_count,
    lr_ref, lengths_ref, slab_ref,
    grads_ref, means_ref,
    box1, box2, box3, box4, rows_out, own_part, own_sem,
    s1, r1, s2, r2, s3, r3, s4, r4,
):
    c = lax.axis_index("corpus")
    d = lax.axis_index("dp")
    tokens = lr_ref.shape[0]
    rank = lr_ref.shape[1] // 2
    share = tokens // corpus_count
    per_prompt = LENGTH // share
    prompts = tokens // LENGTH
    mesh_id = pl.DeviceIdType.MESH
    hops = range(1, corpus_count)
    dp_hops = range(1, dp_count)
    everyone = [(i, j) for i in range(corpus_count) for j in range(dp_count) if (i, j) != (0, 0)]

    def c_of(hop):
        return lax.rem(c + hop, corpus_count)

    def d_of(hop):
        return lax.rem(d + hop, dp_count)

    own_rows = lr_ref.at[pl.ds(pl.multiple_of(c * share, share), share)]
    own_load = pltpu.make_async_copy(own_rows, own_part, own_sem)
    own_load.start()

    barrier = pltpu.get_barrier_semaphore()
    for i, j in everyone:
        pl.semaphore_signal(
            barrier, inc=1, device_id={"corpus": c_of(i), "dp": d_of(j)}, device_id_type=mesh_id
        )
    pl.semaphore_wait(barrier, len(everyone))

    def remote(src, dst, ssem, rsem, where):
        return pltpu.make_async_remote_copy(
            src_ref=src, dst_ref=dst, send_sem=ssem, recv_sem=rsem,
            device_id=where, device_id_type=mesh_id,
        )

    def part_of(who):
        return lr_ref.at[pl.ds(pl.multiple_of(who * share, share), share)]

    sent = []

    def send(*args):
        copy = remote(*args)
        copy.start()
        sent.append(copy)

    for hop in hops:
        send(part_of(c_of(hop)), box1.at[c], s1.at[hop], r1.at[c], {"corpus": c_of(hop)})
    own_load.wait()
    total = own_part[...]
    for hop in hops:
        who = c_of(hop)
        remote(box1.at[who], box1.at[who], s1.at[hop], r1.at[who], {"corpus": who}).wait_recv()
        total += box1[who]

    position = lax.rem(c, per_prompt) * share + lax.broadcasted_iota(jnp.int32, (share, rank), 0)
    used = position < lengths_ref[c // per_prompt]
    left = jnp.where(used, total[:, :rank], 0.0)
    box2[c] = lax.dot_general(
        left, total[:, rank:], (((0,), (0,)), ((), ())),
        precision=lax.Precision.HIGHEST, preferred_element_type=jnp.float32,
    )
    for hop in hops:
        send(box2.at[c], box2.at[c], s2.at[hop], r2.at[c], {"corpus": c_of(hop)})
    for hop in hops:
        who = c_of(hop)
        remote(box2.at[who], box2.at[who], s2.at[hop], r2.at[who], {"corpus": who}).wait_recv()

    for q in range(prompts):
        whole = box2[q * per_prompt]
        for k in range(1, per_prompt):
            whole += box2[q * per_prompt + k]
        for r in range(rank):
            grads_ref[q : q + 1, r * rank : (r + 1) * rank] = whole[r : r + 1, :]

    box3[d] = grads_ref[...]
    for hop in dp_hops:
        send(box3.at[d], box3.at[d], s3.at[hop], r3.at[d], {"dp": d_of(hop)})
    for hop in dp_hops:
        who = d_of(hop)
        remote(box3.at[who], box3.at[who], s3.at[hop], r3.at[who], {"dp": who}).wait_recv()
    queries = jnp.concatenate([box3[k] for k in range(dp_count)], axis=0).astype(jnp.bfloat16)
    scores = lax.dot_general(queries, slab_ref[...], NT, preferred_element_type=jnp.float32)
    scores = scores * (4.0 / math.sqrt(GRAD * LENGTH))
    for k in range(dp_count):
        rows_out[k] = scores[k * prompts : (k + 1) * prompts, :]

    slot = c * dp_count + d
    box4[slot] = rows_out[d]
    for n, (i, j) in enumerate(everyone):
        send(
            rows_out.at[d_of(j)], box4.at[slot], s4.at[n], r4.at[slot],
            {"corpus": c_of(i), "dp": d_of(j)},
        )
    for n, (i, j) in enumerate(everyone):
        other = c_of(i) * dp_count + d_of(j)
        here = box4.at[other]
        remote(here, here, s4.at[n], r4.at[other], {"corpus": c_of(i), "dp": d_of(j)}).wait_recv()

    values = jnp.concatenate([box4[k] for k in range(corpus_count * dp_count)], axis=1)
    top = jnp.max(values, axis=1, keepdims=True)
    taken = jnp.zeros((prompts, 1), jnp.float32)
    total = jnp.zeros((prompts, 1), jnp.float32)
    for n in range(TOPK):
        count = jnp.sum((values == top).astype(jnp.float32), axis=1, keepdims=True)
        use = jnp.minimum(count, TOPK - taken)
        total += use * top
        taken += use
        if n < TOPK - 1:
            top = jnp.max(jnp.where(values < top, values, -3e38), axis=1, keepdims=True)
    means_ref[...] = jnp.broadcast_to(total * (1.0 / TOPK), means_ref.shape)
    for copy in sent:
        copy.wait_send()


def fused_tail(corpus_count, dp_count, left_right, lengths, slab):
    tokens, width = left_right.shape
    rank = width // 2
    prompts = lengths.shape[0]
    examples = slab.shape[0]
    dma = pltpu.SemaphoreType.DMA
    everyone = corpus_count * dp_count
    inside = pl.BlockSpec(memory_space=pltpu.VMEM)
    f32 = jnp.float32
    grads, means = pl.pallas_call(
        functools.partial(tail_kernel, corpus_count, dp_count),
        out_shape=(
            jax.ShapeDtypeStruct((prompts, GRAD), f32),
            jax.ShapeDtypeStruct((prompts, 128), f32),
        ),
        in_specs=[pl.BlockSpec(memory_space=pl.ANY), pl.BlockSpec(memory_space=pltpu.SMEM), inside],
        out_specs=(inside, inside),
        scratch_shapes=[
            pltpu.VMEM((corpus_count, tokens // corpus_count, width), f32),
            pltpu.VMEM((corpus_count, rank, rank), f32),
            pltpu.VMEM((dp_count, prompts, GRAD), f32),
            pltpu.VMEM((everyone, prompts, examples), f32),
            pltpu.VMEM((dp_count, prompts, examples), f32),
            pltpu.VMEM((tokens // corpus_count, width), f32), dma,
            dma((corpus_count,)), dma((corpus_count,)),
            dma((corpus_count,)), dma((corpus_count,)),
            dma((dp_count,)), dma((dp_count,)),
            dma((everyone,)), dma((everyone,)),
        ],
        compiler_params=pltpu.CompilerParams(
            collective_id=1, has_side_effects=True, vmem_limit_bytes=16 * 1024 * 1024
        ),
    )(left_right, lengths, slab)
    return grads, means[:, 0]


def plain_parts(hidden_in, gate_pre, up_out, out_grad, w_down, proj_in, proj_out):
    full_weight = lax.all_gather(w_down, "dp", axis=1, tiled=True)
    grad_hidden = lax.dot_general(
        lax.all_gather(out_grad, "corpus", axis=1, tiled=True),
        full_weight,
        NT,
        preferred_element_type=jnp.float32,
    )
    gate_value = gate_pre.astype(jnp.float32)
    sigmoid_gate = jax.nn.sigmoid(gate_value)
    gate_grad = (
        grad_hidden
        * up_out.astype(jnp.float32)
        * sigmoid_gate
        * (1.0 + gate_value * (1.0 - sigmoid_gate))
    ).astype(jnp.bfloat16)
    left_part = jnp.dot(hidden_in, proj_in, preferred_element_type=jnp.float32)
    right_part = jnp.dot(gate_grad, proj_out, preferred_element_type=jnp.float32)
    return left_part, right_part


def local(fused, corpus_count, hidden_in, gate_pre, up_out, out_grad, w_down, proj_in, proj_out, lengths, slab):
    tok_rows = hidden_in.shape[0]
    query_count = lengths.shape[0]
    layer = (hidden_in, gate_pre, up_out, out_grad, w_down, proj_in, proj_out)
    if fused:
        left_right = fused_parts(corpus_count, *layer)
        return fused_tail(corpus_count, 4, left_right, lengths, slab)
    left_part, right_part = plain_parts(*layer)
    token_index = jnp.arange(tok_rows, dtype=jnp.int32)
    position = token_index % LENGTH
    prompt_of = token_index // LENGTH
    prompt_ids = jnp.arange(query_count, dtype=jnp.int32)
    mask_table = (
        (prompt_of[:, None] == prompt_ids[None, :]) & (position[:, None] < lengths[None, :])
    ).astype(jnp.float32)
    left_all, right_all = lax.psum((left_part, right_part), "corpus")
    example_grads = jnp.einsum(
        "tq,tr,tc->qrc", mask_table, left_all, right_all, precision=lax.Precision.HIGHEST
    )
    query_grads = example_grads.reshape(query_count, GRAD)
    queries = lax.all_gather(query_grads.astype(jnp.bfloat16), "dp", axis=0, tiled=True)
    scores = lax.dot_general(queries, slab, NT, preferred_element_type=jnp.float32)
    scores = scores * (4.0 / math.sqrt(GRAD * LENGTH))
    leaders = lax.top_k(scores, TOPK)[0]
    gathered = lax.all_gather(leaders, ("corpus", "dp"), axis=1, tiled=True)
    leaders = lax.top_k(gathered, TOPK)[0]
    own_rows = lax.dynamic_slice_in_dim(leaders, lax.axis_index("dp") * query_count, query_count, 0)
    return (query_grads, jnp.mean(own_rows, axis=1))


def solution(mesh):
    sizes = dict(mesh.shape)
    fused = sizes["groups"] == 2 and sizes["dp"] == 4 and sizes["corpus"] == 4
    in_specs = (
        P(("groups", "dp"), "corpus"),
        P(("groups", "dp"), "corpus"),
        P(("groups", "dp"), "corpus"),
        P(("groups", "dp"), "corpus"),
        P("corpus", "dp"),
        P("corpus", None),
        P("corpus", None),
        P(("groups", "dp")),
        P(("groups", "corpus", "dp"), None),
    )
    out_specs = (P(("groups", "dp"), None), P(("groups", "dp")))
    return jax.shard_map(
        functools.partial(local, fused, sizes["corpus"]),
        mesh=mesh, in_specs=in_specs, out_specs=out_specs, check_vma=False,
    )
```
